128 devices in a mesh: row: 16 (over y, x_hi, core), col: 8 (over z, x_lo).
Axes of the slice: x: 4 (x_hi: 2, x_lo: 2; x = x_hi * 2 + x_lo), y: 4, z: 4, core: 2. Of those that a mesh axis runs over, the one named last changes fastest.
Arguments:
- tokens: bfloat16 [6144, 6144], P('row'), may hold values from -6 to 6
- ln_gain: float32 [6144], replicated, may hold values from 0.1 to 1.9
- qkv_weight: bfloat16 [6144, 3, 3072], P('row', None, 'col'), may hold values from -0.078125 to 0.078125
- q_gain: float32 [24, 128], P('col'), may hold values from 0.4 to 5
- k_gain: float32 [24, 128], P('col'), may hold values from 0.4 to 5
- block_mask: int32 [24, 48, 48], P('col'), may hold values from 0 to 1, as said below
- out_weight: bfloat16 [3072, 6144], P('row', 'col'), may hold values from -0.875 to 0.875
- grad_out: bfloat16 [6144, 6144], P('row', 'col'), may hold values from -6 to 6
Outputs:
- branch_out: bfloat16 [6144, 6144], P('row', 'col')
- out_weight_grad: float32 [3072, 6144], P('row', 'col')
The draws below stay inside these ranges and needn't reach their ends.
Inputs may be any that keep to these rules, and one draw needn't show every extreme that they name: `block_mask`: entries are 0 or 1; every block sees itself; spectral heads see their spatial window, spatial heads their band group, some heads both, with further blocks scattered at rates that differ by head and by band.
All inputs are finite; a program needn't handle non-finite values.
Results may differ from the reference program's by a relative error of at most 0.014.
The reference program's roundings to bfloat16 on the way (of `normed`, `weights` and `attn`) count: a program that leaves them out, or rounds other values in their place, can miss the bound.
Values may be sent and summed in bfloat16 or wider, within the bound.
No kernel may reach another device: no remote copies, remote signals or barrier semaphores. Data moves between devices by JAX's collectives and lax.ppermute only.
A program may use at most 128 MiB of HBM per device.

```python
import jax
import jax.numpy as jnp
from jax import lax

D = 6144
HS = 128
HEADS = 24
HD = 3072
TOKENS = 6144
BLOCK = 128
BANDS = 8


def draw_block_mask(key, part):
    nblocks = TOKENS // BLOCK
    key_kind, key_rate, key_extra = jax.random.split(key, 3)
    head_kind = jax.random.randint(key_kind, (HEADS,), 0, 3)
    rate_base = jax.random.randint(key_rate, (HEADS,), 1, 6)
    block_ids = jnp.arange(nblocks, dtype=jnp.int32)
    band_id = block_ids % BANDS
    window = block_ids // BANDS
    same_window = (window[:, None] == window[None, :])[None]
    same_band = (band_id[:, None] == band_id[None, :])[None]
    kind_grid = head_kind[:, None, None]
    base_mask = jnp.where(kind_grid == 0, same_window, jnp.where(kind_grid == 1, same_band, same_window | same_band))
    threshold = rate_base[:, None, None] * (1 + band_id[None, :, None] % 4)
    extra = jax.random.randint(key_extra, (HEADS, nblocks, nblocks), 0, 32) < threshold
    diagonal = (block_ids[:, None] == block_ids[None, :])[None]
    return (base_mask | extra | diagonal).astype(jnp.int32)


def gain_draw(key):
    return 1.0 + 0.3 * jnp.clip(jax.random.normal(key, (HEADS, HS), jnp.float32), -2.0, 2.0)


def draw_q_gain(key, part):
    return gain_draw(jax.random.fold_in(key, 11))


def draw_k_gain(key, part):
    return gain_draw(jax.random.fold_in(key, 23))


def level_of(own_key, dims, shards, low, top_value):
    factor_of, own = 1.0, jax.random.fold_in(own_key, 6)
    for axis_at, parts in shards:
        heights = jnp.exp(jax.random.uniform(jax.random.fold_in(own, axis_at), (parts,), jnp.float32, low / len(shards), top_value / len(shards)))
        factor_of = factor_of * jnp.repeat(heights, dims[axis_at] // parts).reshape([-1 if axis == axis_at else 1 for axis in range(len(dims))])
    return factor_of


def scatter_about(stream_key, dims, width, most, pieces=(), kind=jnp.bfloat16):
    result = jax.random.normal(stream_key, dims, jnp.float32) * width
    if len(pieces) > 0:
        result = level_of(stream_key, dims, pieces, -0.22, 0.18) * result
    return jnp.clip(result, min=-most, max=most).astype(kind)


def setup_inputs(seed: int = 0) -> dict:
    seeds = jax.random.split(jax.random.key(seed), 9)
    return {
        "tokens": scatter_about(seeds[0], (TOKENS, D), 1.0, 6.0, ((0, 16),)),
        "ln_gain": jnp.clip(1.0 + 0.18 * jax.random.normal(seeds[1], (D,), jnp.float32), 0.1, 1.9),
        "qkv_weight": scatter_about(seeds[2], (D, 3, HD), D ** -0.5, 0.078125, ((0, 16), (2, 8))),
        "q_gain": draw_q_gain(jax.random.fold_in(seeds[8], 71), 0),
        "k_gain": draw_k_gain(jax.random.fold_in(seeds[8], 71), 0),
        "block_mask": draw_block_mask(jax.random.fold_in(seeds[8], 71), 0),
        "out_weight": scatter_about(seeds[6], (HD, D), (HD // 64) ** -0.5, 0.875, ((0, 16), (1, 8))),
        "grad_out": scatter_about(seeds[7], (TOKENS, D), 1.0, 6.0, ((0, 16), (1, 8))),
    }


EPS = 1e-06

def norm_rows(values, gain):
    center = lax.optimization_barrier(jnp.mean(values, axis=-1, keepdims=True))
    shifted = values - center
    variance = lax.optimization_barrier(jnp.mean(shifted * shifted, axis=-1, keepdims=True))
    return shifted * lax.rsqrt(variance + EPS) * gain

def reference(tokens, ln_gain, qkv_weight, q_gain, k_gain, block_mask, out_weight, grad_out):
    normed = norm_rows(tokens.astype(jnp.float32), ln_gain).astype(jnp.bfloat16)
    flat_weight = qkv_weight.reshape(D, 3 * HD)
    mixed = jnp.dot(normed, flat_weight, preferred_element_type=jnp.float32).reshape(TOKENS, 3, HEADS, HS)
    queries = norm_rows(mixed[:, 0], q_gain).astype(jnp.bfloat16)
    keys_all = norm_rows(mixed[:, 1], k_gain).astype(jnp.bfloat16)
    values_all = mixed[:, 2].astype(jnp.bfloat16)
    nblocks = TOKENS // BLOCK
    score_scale = HS ** (-0.5)

    def one_head(operands):
        query_head, key_head, value_head, mask_head = operands
        scores = jnp.dot(query_head, key_head.T, preferred_element_type=jnp.float32) * score_scale
        scores = scores.reshape(nblocks, BLOCK, nblocks, BLOCK)
        is_live = mask_head[:, None, :, None] > 0
        scores = jnp.where(is_live, scores, -1e+30)
        top_score = lax.optimization_barrier(jnp.max(scores, axis=(2, 3), keepdims=True))
        expo = jnp.where(is_live, jnp.exp(scores - top_score), 0.0)
        denom = lax.optimization_barrier(jnp.sum(expo, axis=(2, 3))).reshape(TOKENS, 1)
        weights = expo.reshape(TOKENS, TOKENS).astype(jnp.bfloat16)
        return (jnp.dot(weights, value_head, preferred_element_type=jnp.float32) / denom).astype(jnp.bfloat16)
    per_head = lax.map(one_head, (queries.transpose(1, 0, 2), keys_all.transpose(1, 0, 2), values_all.transpose(1, 0, 2), block_mask))
    attn = per_head.transpose(1, 0, 2).reshape(TOKENS, HD)
    branch_out = jnp.dot(attn, out_weight, preferred_element_type=jnp.float32).astype(jnp.bfloat16)
    out_weight_grad = jnp.dot(attn.T, grad_out, preferred_element_type=jnp.float32)
    return (branch_out, out_weight_grad)
```

```python
import functools

import jax
import jax.numpy as jnp
from jax import lax
from jax.experimental import pallas as pl
from jax.experimental.pallas import tpu as pltpu
from jax.sharding import PartitionSpec as P

HS = 128
BLOCK = 128
EPS = 1e-06
ROWS, COLS = 16, 8
NY, NZ = 4, 4
SPLIT = 512
GROUP = 4
NEG = -1e30


VMEM = pl.BlockSpec(memory_space=pltpu.VMEM)
SMEM = pl.BlockSpec(memory_space=pltpu.SMEM)
ANY = pl.BlockSpec(memory_space=pl.ANY)

FULL = [(0, 0), (0, 1), (1, 0), (3, 0), (2, 0)]
CUT = [(1, 1), (3, 1), (2, 1)]


def row_perm(dy, flip):
    return [(r, (((r // 4 + dy) % NY) * 4 + r % 4) ^ flip) for r in range(ROWS)]


def col_perm(dz, flip):
    return [(c, (((c // 2 + dz) % NZ) * 2 + c % 2) ^ flip) for c in range(COLS)]


def row_send(x, dy, flip):
    return lax.ppermute(x, "row", row_perm(dy, flip))


def norm_rows(values, gain):
    center = jnp.mean(values, axis=-1, keepdims=True)
    shifted = values - center
    variance = jnp.mean(shifted * shifted, axis=-1, keepdims=True)
    return shifted * lax.rsqrt(variance + EPS) * gain


def gather_rows(own):
    got = {(0, 0, 0): (own,)}
    got[0, 1, 0] = (row_send(own, 0, 2),)
    for dy in (1, 3, 2):
        got[dy, 0, 0] = (row_send(own, dy, 0),)
    across = got[0, 1, 0][0][:SPLIT]
    for dy in (1, 3, 2):
        top = row_send(across, dy, 0)
        bottom = row_send(got[dy, 0, 0][0][SPLIT:], 0, 2)
        got[dy, 1, 0] = (top, bottom)
    for dy, hx in FULL + CUT:
        got[dy, hx, 1] = tuple(row_send(part, 0, 1) for part in got[dy, hx, 0])
    return got


def source_of(row, dy, hx, cx):
    y, rest = row // 4, row % 4
    return ((y + NY - dy) % NY) * 4 + jnp.bitwise_xor(rest, 2 * hx + cx)


def spans(parts, start, stop):
    if len(parts) == 1:
        return [(0, start, stop - start, 0)]
    found = []
    if start < SPLIT:
        found.append((0, start, min(stop, SPLIT) - start, 0))
    if stop > SPLIT:
        low = max(start, SPLIT)
        found.append((1, low - SPLIT, stop - low, low - start))
    return found


def project_kernel(layout, first, last, *refs):
    refs = list(refs)
    src_ref, x_ref = refs.pop(0), refs.pop(0)
    pieces = [[refs.pop(0) for _ in range(n)] for n in layout]
    if not first:
        acc_in = refs.pop(0)
    if last:
        qg_ref, kg_ref, wo_ref, q_ref, pay_ref = (refs.pop(0) for _ in range(5))
    else:
        acc_out = refs.pop(0)
    acc = refs.pop(0)
    bufs = [[refs.pop(0) for _ in range(n)] for n in layout]
    sems = refs.pop(0)
    copies, at = [], 0
    for piece, buf in zip(pieces, bufs):
        row = []
        for a, b in zip(piece, buf):
            row.append(pltpu.make_async_copy(a, b, sems.at[at]))
            at += 1
        copies.append(row)
    for row in copies:
        for copy in row:
            copy.start()
    width = acc.shape[2]
    for i, buf in enumerate(bufs):
        for copy in copies[i]:
            copy.wait()
        cols = pl.ds(pl.multiple_of(src_ref[i] * width, 128), width)
        x = x_ref[:, cols]
        for part in range(3):
            total = None
            for which, at, rows, off in spans(buf, part * width, (part + 1) * width):
                one = jnp.dot(
                    x[:, off : off + rows],
                    buf[which][at : at + rows, :],
                    preferred_element_type=jnp.float32,
                )
                total = one if total is None else total + one
            if i == 0 and first:
                acc[part] = total
            elif i == 0:
                acc[part] = acc_in[part] + total
            else:
                acc[part] = acc[part] + total
    if not last:
        acc_out[...] = acc[...]
        return
    for head in range(width // HS):
        lanes = slice(head * HS, (head + 1) * HS)
        q_ref[:, lanes] = norm_rows(acc[0, :, lanes], qg_ref[head : head + 1, :]).astype(jnp.bfloat16)
        pay_ref[0:width, lanes] = norm_rows(acc[1, :, lanes], kg_ref[head : head + 1, :]).astype(
            jnp.bfloat16
        )
    pay_ref[width : 2 * width, :] = acc[2].astype(jnp.bfloat16)
    half = wo_ref.shape[0]
    pay_ref[2 * width : 2 * width + half, :] = wo_ref[:, :width]
    pay_ref[2 * width + half :, :] = wo_ref[:, width:]


def project(src, normed, pieces, acc=None, tail=None):
    rows, width = normed.shape[0], pieces[0][0].shape[1]
    layout = [len(p) for p in pieces]
    flat = [part for piece in pieces for part in piece]
    operands = [src, normed, *flat]
    in_specs = [SMEM, VMEM] + [ANY] * len(flat)
    aliases = {}
    if acc is not None:
        operands.append(acc)
        in_specs.append(VMEM)
    shape = jax.ShapeDtypeStruct((3, rows, width), jnp.float32)
    if tail is not None:
        operands += list(tail)
        in_specs += [VMEM] * 3
        out_shape = (
            jax.ShapeDtypeStruct((rows, width), jnp.bfloat16),
            jax.ShapeDtypeStruct((3 * width, width), jnp.bfloat16),
        )
        out_specs = (VMEM, VMEM)
    else:
        out_shape, out_specs = shape, VMEM
    return pl.pallas_call(
        functools.partial(project_kernel, layout, acc is None, tail is not None),
        out_shape=out_shape,
        in_specs=in_specs,
        out_specs=out_specs,
        scratch_shapes=[pltpu.VMEM(shape.shape, jnp.float32)]
        + [pltpu.VMEM(p.shape, p.dtype) for p in flat]
        + [pltpu.SemaphoreType.DMA((len(flat),))],
        cost_estimate=pl.CostEstimate(
            flops=2 * rows * width * 3 * width * len(layout),
            bytes_accessed=sum(p.size * 2 for p in flat) + 2 * shape.size * 4,
            transcendentals=0,
        ),
        name="project",
    )(*operands)


def attend_kernel(layout, heads, *refs):
    refs = list(refs)
    src_ref, count_ref, list_ref, q_ref = (refs.pop(0) for _ in range(4))
    pieces = [[refs.pop(0) for _ in range(n)] for n in layout]
    out_ref = refs.pop(0)
    keys, values, scores, sems = refs
    width = q_ref.shape[1]
    copies, at = [], 0
    for i, piece in enumerate(pieces):
        base = pl.multiple_of(src_ref[i] * width, 128)
        for target, start in ((keys, 0), (values, width)):
            for which, row, rows, off in spans(piece, start, start + width):
                copies.append(
                    pltpu.make_async_copy(
                        piece[which].at[pl.ds(row, rows), :],
                        target.at[pl.ds(base + off, rows), :],
                        sems.at[at],
                    )
                )
                at += 1
    for copy in copies:
        copy.start()
    for copy in copies:
        copy.wait()
    qblocks = q_ref.shape[0] // BLOCK
    scale = HS**-0.5
    for head in range(heads):
        lanes = slice(head * HS, (head + 1) * HS)

        def one_block(a, carry):
            unit = head * qblocks + a
            n = count_ref[unit]
            steps = (n + GROUP - 1) // GROUP
            rows = pl.ds(pl.multiple_of(a * BLOCK, BLOCK), BLOCK)
            q = q_ref[rows, lanes]

            def block_of(ref, at):
                return ref[pl.ds(pl.multiple_of(list_ref[unit, at] * BLOCK, BLOCK), BLOCK), lanes]

            def score(step, top):
                k = jnp.concatenate([block_of(keys, step * GROUP + j) for j in range(GROUP)], axis=0)
                s = lax.dot_general(
                    q, k, (((1,), (1,)), ((), ())), preferred_element_type=jnp.float32
                )
                for j in range(GROUP):
                    bias = jnp.where(step * GROUP + j < n, 0.0, NEG)
                    part = s[:, j * BLOCK : (j + 1) * BLOCK] + bias
                    scores[step, :, j * BLOCK : (j + 1) * BLOCK] = part
                    top = jnp.maximum(top, part)
                return top

            top = lax.fori_loop(0, steps, score, jnp.full((BLOCK, BLOCK), NEG, jnp.float32))
            top = jnp.max(top, axis=-1, keepdims=True)

            def gather(step, carry):
                accum, denom = carry
                expo = jnp.exp((scores[step] - top) * scale)
                for j in range(GROUP):
                    denom = denom + expo[:, j * BLOCK : (j + 1) * BLOCK]
                v = jnp.concatenate([block_of(values, step * GROUP + j) for j in range(GROUP)], axis=0)
                accum = accum + jnp.dot(
                    expo.astype(jnp.bfloat16), v, preferred_element_type=jnp.float32
                )
                return accum, denom

            zero = jnp.zeros((BLOCK, BLOCK), jnp.float32)
            accum, denom = lax.fori_loop(0, steps, gather, (zero, zero))
            denom = jnp.sum(denom, axis=-1, keepdims=True)
            out_ref[rows, lanes] = (accum / denom).astype(jnp.bfloat16)
            return carry

        lax.fori_loop(0, qblocks, one_block, 0)


def attend(src, counts, lists, queries, pieces, heads):
    rows, width = queries.shape
    layout = [len(p) for p in pieces]
    flat = [part for piece in pieces for part in piece]
    tokens = len(pieces) * rows
    blocks = tokens // BLOCK
    ncopies = sum(len(spans(p, s, s + width)) for p in pieces for s in (0, width))
    return pl.pallas_call(
        functools.partial(attend_kernel, layout, heads),
        out_shape=jax.ShapeDtypeStruct((rows, width), jnp.bfloat16),
        in_specs=[SMEM, SMEM, SMEM, VMEM] + [ANY] * len(flat),
        out_specs=VMEM,
        scratch_shapes=[
            pltpu.VMEM((tokens, width), jnp.bfloat16),
            pltpu.VMEM((tokens, width), jnp.bfloat16),
            pltpu.VMEM((blocks // GROUP, BLOCK, GROUP * BLOCK), jnp.float32),
            pltpu.SemaphoreType.DMA((ncopies,)),
        ],
        cost_estimate=pl.CostEstimate(
            flops=4 * rows * width * tokens,
            bytes_accessed=4 * tokens * width,
            transcendentals=rows * heads * tokens,
        ),
        name="attend",
    )(src, counts, lists, queries, *flat)


def grad_kernel(slot_ref, core_ref, grad_ref, *refs):
    pieces, keep_ref, send_ref, buf = refs[:COLS], refs[COLS], refs[COLS + 1], refs[COLS + 2]
    half = keep_ref.shape[1]
    core = core_ref[0]
    mine = pl.ds(pl.multiple_of(core * half, 64), half)
    other = pl.ds(pl.multiple_of((1 - core) * half, 64), half)
    grad = grad_ref[...]
    for i, piece in enumerate(pieces):
        buf[...] = lax.dot_general(
            piece[...], grad, (((0,), (0,)), ((), ())), preferred_element_type=jnp.float32
        )
        keep_ref[slot_ref[i]] = buf[mine, :]
        send_ref[slot_ref[i]] = buf[other, :].astype(jnp.bfloat16)


def grad_partials(slots, core, grad, pieces):
    rows, width = pieces[0].shape
    out = grad.shape[1]
    half = width // 2
    return pl.pallas_call(
        grad_kernel,
        out_shape=(
            jax.ShapeDtypeStruct((COLS, half, out), jnp.float32),
            jax.ShapeDtypeStruct((COLS, half, out), jnp.bfloat16),
        ),
        in_specs=[SMEM, SMEM] + [VMEM] * (1 + COLS),
        out_specs=(VMEM, VMEM),
        scratch_shapes=[pltpu.VMEM((width, out), jnp.float32)],
        cost_estimate=pl.CostEstimate(
            flops=2 * rows * width * COLS * out, bytes_accessed=16 << 20, transcendentals=0
        ),
        name="grad",
    )(slots, core, grad, *pieces)


def branch_kernel(layout, width, *refs):
    refs = list(refs)
    src_ref, col_ref = refs.pop(0), refs.pop(0)
    attn = [refs.pop(0) for _ in range(COLS)]
    pieces = [[refs.pop(0) for _ in range(n)] for n in layout]
    out_ref, weight, sems = refs
    half = width // 2
    copies = []
    for i, piece in enumerate(pieces):
        for side in range(2):
            start = 2 * width + side * half
            ((which, row, rows, _),) = spans(piece, start, start + half)
            copies.append(
                pltpu.make_async_copy(
                    piece[which].at[pl.ds(row, rows), :],
                    weight.at[side, pl.ds(pl.multiple_of(src_ref[i] * half, 64), half), :],
                    sems.at[len(copies)],
                )
            )
    for copy in copies:
        copy.start()
    for copy in copies:
        copy.wait()
    for side in range(2):
        total = None
        for i, piece in enumerate(attn):
            rows = pl.ds(pl.multiple_of(col_ref[i] * width, 128), width)
            one = jnp.dot(piece[...], weight[side, rows, :], preferred_element_type=jnp.float32)
            total = one if total is None else total + one
        out_ref[:, side * width : (side + 1) * width] = total.astype(jnp.bfloat16)


def branch_out(src, cols, attn, pieces):
    rows, width = attn[0].shape
    layout = [len(p) for p in pieces]
    flat = [part for piece in pieces for part in piece]
    return pl.pallas_call(
        functools.partial(branch_kernel, layout, width),
        out_shape=jax.ShapeDtypeStruct((rows, 2 * width), jnp.bfloat16),
        in_specs=[SMEM, SMEM] + [VMEM] * COLS + [ANY] * len(flat),
        out_specs=VMEM,
        scratch_shapes=[
            pltpu.VMEM((2, COLS * width, width), jnp.bfloat16),
            pltpu.SemaphoreType.DMA((2 * len(pieces),)),
        ],
        cost_estimate=pl.CostEstimate(
            flops=4 * rows * width * COLS * width, bytes_accessed=10 << 20, transcendentals=0
        ),
        name="branch",
    )(src, cols, *attn, *flat)


def per_device(tokens, ln_gain, qkv_weight, q_gain, k_gain, block_mask, out_weight, grad_out):
    rows = tokens.shape[0]
    heads = q_gain.shape[0]
    width = heads * HS
    row, col = lax.axis_index("row"), lax.axis_index("col")
    order = [(dy, hx, cx) for dy, hx in FULL + CUT for cx in (0, 1)]
    src = jnp.stack([source_of(row, *o) for o in order]).astype(jnp.int32)

    weight = qkv_weight.transpose(1, 0, 2).reshape(3 * qkv_weight.shape[0], width)
    got = gather_rows(weight)
    normed = norm_rows(tokens.astype(jnp.float32), ln_gain).astype(jnp.bfloat16)

    qblocks = rows // BLOCK
    nblocks = block_mask.shape[1]
    seen = lax.dynamic_slice_in_dim(block_mask, row * qblocks, qblocks, 1) > 0
    seen = seen.reshape(heads * qblocks, nblocks)
    ids = jnp.arange(nblocks, dtype=jnp.int32)
    before = jnp.sum(
        jnp.where(seen[:, None, :] & (ids[None, None, :] < ids[None, :, None]), 1, 0), axis=-1
    )
    counts = jnp.sum(seen.astype(jnp.int32), axis=-1)
    hit = seen[:, None, :] & (before[:, None, :] == ids[None, :, None])
    lists = jnp.sum(jnp.where(hit, ids[None, None, :], 0), axis=-1)

    def at(keys):
        return [got[k] for k in keys]

    acc = project(src[:4], normed, at(order[:4]))
    acc = project(src[4:10], normed, at(order[4:10]), acc)
    queries, payload = project(
        src[10:], normed, at(order[10:]), acc, (q_gain, k_gain, out_weight)
    )
    got = gather_rows(payload)
    pieces = at(order)
    attn_here = attend(src, counts, lists, queries, pieces, heads)

    steps = [(dz, fl) for dz in (0, 1, 3, 2) for fl in (0, 1)]
    attn, cols, slots = [], [], []
    y, h = row // 4, (row // 2) % 2
    for dz, fl in steps:
        attn.append(
            attn_here if (dz, fl) == (0, 0) else lax.ppermute(attn_here, "col", col_perm(dz, fl))
        )
        z_of, l_of = (col // 2 + NZ - dz) % NZ, jnp.bitwise_xor(col % 2, fl)
        cols.append(z_of * 2 + l_of)
        slots.append(((z_of + NY - y) % NY) * 2 + jnp.bitwise_xor(l_of, h))
    cols = jnp.stack(cols).astype(jnp.int32)
    slots = jnp.stack(slots).astype(jnp.int32)
    core = (row % 2).astype(jnp.int32).reshape(1)
    keep, send = grad_partials(slots, core, grad_out, attn)
    came = row_send(send, 0, 1)
    total = keep[0] + came[0].astype(jnp.float32)
    for dy in (2, 1, 3, 0):
        for hx in (1, 0):
            if (dy, hx) == (0, 0):
                continue
            slot = dy * 2 + hx
            chip = (keep[slot] + came[slot].astype(jnp.float32)).astype(jnp.bfloat16)
            total = total + row_send(chip, dy, 2 * hx).astype(jnp.float32)
    branch = branch_out(src, cols, attn, pieces)
    return branch, total


def solution(mesh):
    in_specs = (
        P("row", None),
        P(),
        P("row", None, "col"),
        P("col", None),
        P("col", None),
        P("col", None, None),
        P("row", "col"),
        P("row", "col"),
    )
    out_specs = (P("row", "col"), P("row", "col"))
    return jax.shard_map(
        per_device, mesh=mesh, in_specs=in_specs, out_specs=out_specs, check_vma=False
    )
```
